32 devices in a mesh: beam: 2 (over y), freq: 8 (over z, x), tm: 2 (over core).
Axes of the slice: x: 2, y: 2, z: 4, core: 2. Of those that a mesh axis runs over, the one named last changes fastest.
Arguments:
- intensity: float32 [128, 8192], P(('beam', 'freq'), 'tm'), parts along dimension 0, may hold values from -6 to 6
- channel_shift: int32 [64, 2], replicated, may hold values from 0 to 15, as said below
- section_shift: int32 [6, 128], replicated, may hold values from 0 to 96, as said below
- filter_bank: float32 [8, 128], replicated, may hold values from -0.5 to 0.5
Outputs:
- power_map: float32 [256, 8, 8], P(('beam', 'freq'), None, 'tm'), parts along dimension 0
The draws below stay inside these ranges and needn't reach their ends.
There are 2 independent parts, one for each index of `beam`. The reference program is written for one: setup_inputs(seed, part) draws one part's arguments, and reference() takes and returns one part's arrays. A program takes and returns all parts, laid end to end along the dimension named above; an argument that names none is the same for every part. Nothing has to cross between parts.
Inputs may be any that keep to these rules, and one draw needn't show every extreme that they name: `channel_shift`: every entry is at most 15, and some entry equals 15. `section_shift`: every entry of row s lies between 0 and 3 * 2^s, and some entry of each row s equals 3 * 2^s.
All inputs are finite; a program needn't handle non-finite values.
Results may differ from the reference program's by a relative error of at most 0.0003.
Values sent between devices are 32-bit elements; how exact they have to be, the bound alone decides.
No kernel may reach another device: no remote copies, remote signals or barrier semaphores. Data moves between devices by JAX's collectives and lax.ppermute only.
A program may use at most 64 MiB of HBM per device.

```python
from functools import partial
import jax
import jax.numpy as jnp
from jax import lax

CHANNELS = 64
SECTIONS = 6
CH_TRIALS = 2
TRIALS = 128
TIME = 8192
SHIFT_UNIT = 3
CHAN_MAX = 15
TAPS = 128
FILTERS = 8
BLOCK = 1024


def draw_channel_shift(key, part):
    key_values, key_spot = jax.random.split(key)
    values = jax.random.randint(key_values, (CHANNELS, CH_TRIALS), 0, CHAN_MAX + 1)
    chosen_spot = jax.random.randint(key_spot, (), 0, CHANNELS * CH_TRIALS)
    positions = jnp.arange(CHANNELS * CH_TRIALS, dtype=jnp.int32).reshape(CHANNELS, CH_TRIALS)
    return jnp.where(positions == chosen_spot, CHAN_MAX, values).astype(jnp.int32)


def draw_section_shift(key, part):
    key_values, key_spot = jax.random.split(key)
    section_caps = SHIFT_UNIT * 2 ** jnp.arange(SECTIONS, dtype=jnp.int32)
    values = jax.random.randint(key_values, (SECTIONS, TRIALS), 0, 2 ** 30) % (section_caps[:, None] + 1)
    chosen_spot = jax.random.randint(key_spot, (SECTIONS, 1), 0, TRIALS)
    positions = jnp.arange(TRIALS, dtype=jnp.int32)[None, :]
    return jnp.where(positions == chosen_spot, section_caps[:, None], values).astype(jnp.int32)


def steps_of(own_key, dims, shards, least, high):
    def one(dim, parts):
        draws = jax.random.uniform(jax.random.fold_in(jax.random.fold_in(own_key, 6), dim), (parts,), jnp.float32, least / len(shards), high / len(shards))
        return jnp.repeat(jnp.exp(draws), dims[dim] // parts).reshape((-1,) + (1,) * (len(dims) - dim - 1))

    loudness = one(*shards[0])
    for cut in shards[1:]:
        loudness = loudness * one(*cut)
    return loudness


def centred(rng, extent, spread, bound, cuts=(), kind=jnp.bfloat16):
    entries = spread * jax.random.normal(rng, extent, jnp.float32)
    if cuts:
        entries = entries * steps_of(rng, extent, cuts, -0.22, 0.18)
    return jnp.clip(entries, -bound, bound).astype(kind)


def setup_inputs(seed: int = 0, part: int = 0) -> dict:
    keys = jax.random.split(jax.random.key(seed), 5)
    part_keys = jax.random.split(jax.random.fold_in(keys[4], part), 5)
    return {
        "intensity": centred(part_keys[0], (CHANNELS, TIME), 1.0, 6.0, ((0, 8), (1, 2)), jnp.float32),
        "channel_shift": draw_channel_shift(jax.random.fold_in(keys[4], 71), part),
        "section_shift": draw_section_shift(jax.random.fold_in(keys[4], 71), part),
        "filter_bank": centred(keys[3], (FILTERS, TAPS), TAPS ** -0.5, 0.5, (), jnp.float32),
    }


def take_window(one_row, amount, length):
    return lax.dynamic_slice_in_dim(one_row, amount.astype(jnp.int32), length)


def shifted_rows(row_block, shifts, length):
    return jax.vmap(partial(take_window, length=length))(row_block, shifts)


def merge_bands(lower_band, upper_ext, shift_table, out_len):
    doubled_low = jnp.concatenate([lower_band, lower_band], axis=1)[:, :, :out_len]
    doubled_up = jnp.concatenate([upper_ext, upper_ext], axis=1)
    shifted = shifted_rows(doubled_up.reshape(-1, doubled_up.shape[2]), shift_table.reshape(-1), out_len)
    return doubled_low + shifted.reshape(doubled_low.shape)


def reference(intensity, channel_shift, section_shift, filter_bank):
    channels, total_time = intensity.shape
    trials_each = channel_shift.shape[1]
    padded = jnp.concatenate([intensity, jnp.zeros((channels, CHAN_MAX), intensity.dtype)], axis=1)
    tree_rows = shifted_rows(jnp.repeat(padded, trials_each, axis=0), channel_shift.reshape(-1), total_time)
    tree_rows = tree_rows.reshape(channels, trials_each, total_time)
    for section_index in range(SECTIONS):
        max_shift = SHIFT_UNIT * 2 ** section_index
        band_count, band_rows, span_len = tree_rows.shape
        lower_band = tree_rows[0::2]
        upper_band = tree_rows[1::2]
        upper_ext = jnp.concatenate([upper_band, jnp.zeros((band_count // 2, band_rows, max_shift), tree_rows.dtype)], axis=2)
        shift_table = section_shift[section_index].reshape(band_count // 2, 2 * band_rows)
        tree_rows = merge_bands(lower_band, upper_ext, shift_table, total_time)
    dedispersed = tree_rows.reshape(-1, total_time)
    row_count = dedispersed.shape[0]
    fft_size = 2 * total_time
    spectrum = jnp.fft.rfft(dedispersed, n=fft_size, axis=1)

    def one_filter(kernel):
        kernel_spec = jnp.fft.rfft(kernel, n=fft_size)
        series = jnp.fft.irfft(spectrum * jnp.conj(kernel_spec)[None, :], n=fft_size, axis=1)[:, :total_time]
        return jnp.sum((series * series).reshape(row_count, total_time // BLOCK, BLOCK), axis=2)

    power_map = lax.map(one_filter, filter_bank)
    return jnp.transpose(power_map, (1, 0, 2)) / (BLOCK * CHANNELS)
```

```python
from functools import partial

import jax
import jax.numpy as jnp
from jax import lax
from jax.experimental import pallas as pl
from jax.experimental.pallas import tpu as pltpu
from jax.sharding import PartitionSpec as P

SHIFT_UNIT = 3
CHAN_MAX = 15
BLOCK = 1024


def from_behind(block, axis, distance):
    devices = range(lax.axis_size(axis))
    route = [(i - distance, i) for i in devices if i - distance in devices]
    return lax.ppermute(block, axis, route)


def from_partner(array, axis, distance):
    return lax.ppermute(array, axis, [(i, i ^ 1 << distance) for i in range(lax.axis_size(axis))])


def shifted_rows(row_block, shifts, length):
    extra = row_block.shape[1] - length
    bit_count = max(extra, 0).bit_length()
    target = length + 2**bit_count - 1
    current = row_block
    if target > row_block.shape[1]:
        current = jnp.concatenate(
            [
                row_block,
                jnp.zeros((row_block.shape[0], target - row_block.shape[1]), row_block.dtype),
            ],
            axis=1,
        )
    for bit_index in range(bit_count - 1, -1, -1):
        step = 2**bit_index
        chosen = jnp.bitwise_and(jnp.right_shift(shifts, bit_index), 1)[:, None] == 1
        current = jnp.where(chosen, current[:, step:], current[:, : current.shape[1] - step])
    return current


def merge_bands(lower_band, upper_ext, shift_table, out_len):
    doubled_low = jnp.concatenate([lower_band, lower_band], axis=1)[:, :, :out_len]
    doubled_up = jnp.concatenate([upper_ext, upper_ext], axis=1)
    shifted = shifted_rows(
        doubled_up.reshape(-1, doubled_up.shape[2]), shift_table.reshape(-1), out_len
    )
    return doubled_low + shifted.reshape(doubled_low.shape)


def toeplitz_pair(filter_bank):
    filters, tap_count = filter_bank.shape
    period = 2 * tap_count + 1
    padded = jnp.concatenate(
        [filter_bank, jnp.zeros((filters, period - tap_count), filter_bank.dtype)], axis=1
    )
    tiled = jnp.broadcast_to(padded[:, None, :], (filters, tap_count, period))
    flat = tiled.reshape(filters, -1)[:, : 2 * tap_count * tap_count]
    table = jnp.swapaxes(flat.reshape(filters, tap_count, 2 * tap_count), 1, 2)
    return (table[:, :tap_count], table[:, tap_count:])


def body(intensity, channel_shift, section_shift, filter_bank):
    chan_dev, samples = intensity.shape
    n_freq = lax.axis_size("freq")
    local_levels = chan_dev.bit_length() - 1
    freq_levels = n_freq.bit_length() - 1
    trials_each = channel_shift.shape[1]
    row_count = trials_each * chan_dev
    channels = chan_dev * n_freq
    freq_place = lax.axis_index("freq")
    own_section = lax.dynamic_slice_in_dim(section_shift, freq_place * row_count, row_count, 1)
    local_margin = SHIFT_UNIT * (2**local_levels - 1)
    margin = CHAN_MAX + local_margin
    rim_cols = from_behind(intensity[:, :margin], "tm", -1)
    extended = jnp.concatenate([intensity, rim_cols], axis=1)
    own_chan_shift = lax.dynamic_slice_in_dim(channel_shift, freq_place * chan_dev, chan_dev, 0)
    length = samples + margin - CHAN_MAX
    tree_rows = shifted_rows(
        jnp.repeat(extended, trials_each, axis=0), own_chan_shift.reshape(-1), length
    )
    tree_rows = tree_rows.reshape(chan_dev, trials_each, length)
    for section_index in range(local_levels):
        max_shift = SHIFT_UNIT * 2**section_index
        band_count, band_rows, span_len = tree_rows.shape
        lower_band = tree_rows[0::2]
        upper_band = tree_rows[1::2]
        out_len = span_len - max_shift
        upper_ext = upper_band
        shift_table = own_section[section_index].reshape(band_count // 2, 2 * band_rows)
        tree_rows = merge_bands(lower_band, upper_ext, shift_table, out_len)
    own_rows = tree_rows.reshape(row_count, samples)
    first_cross = 0
    for section_index in range(first_cross, freq_levels):
        max_shift = SHIFT_UNIT * 2 ** (local_levels + section_index)
        shift_table = own_section[local_levels + section_index]
        upper_bit = jnp.bitwise_and(jnp.right_shift(freq_place, section_index), 1)
        is_upper = upper_bit == 1
        sent_rows = own_rows
        partner_rows = from_partner(sent_rows, "freq", section_index)
        lower_band = jnp.where(is_upper, partner_rows, sent_rows)
        upper_band = jnp.where(is_upper, sent_rows, partner_rows)
        upper_rim = from_behind(upper_band[:, :max_shift], "tm", -1)
        upper_ext = jnp.concatenate([upper_band, upper_rim], axis=1)
        own_rows = lower_band + shifted_rows(upper_ext, shift_table, samples)
    tap_count = filter_bank.shape[1]
    filters = filter_bank.shape[0]
    tail_rows = from_behind(own_rows[:, : tap_count - 1], "tm", -1)
    padded = jnp.concatenate(
        [own_rows, tail_rows, jnp.zeros((row_count, 1), own_rows.dtype)], axis=1
    )
    first_half = padded[:, :samples].reshape(-1, tap_count)
    second_half = padded[:, tap_count:].reshape(-1, tap_count)
    toep_top, toep_low = toeplitz_pair(filter_bank)
    outputs = []
    for filter_index in range(filters):
        series = jnp.dot(
            first_half,
            toep_top[filter_index],
            precision=lax.Precision.HIGHEST,
            preferred_element_type=jnp.float32,
        )
        series = series + jnp.dot(
            second_half,
            toep_low[filter_index],
            precision=lax.Precision.HIGHEST,
            preferred_element_type=jnp.float32,
        )
        energy = jnp.sum((series * series).reshape(row_count, samples // BLOCK, BLOCK), axis=2)
        outputs.append(energy)
    return jnp.stack(outputs, axis=1) / (BLOCK * channels)


LANES = 128
GROUP = 8


def lane_shift(tiles, amount, count):
    lane = lax.broadcasted_iota(jnp.int32, (GROUP, LANES), 1)
    source = lane + amount
    inside = source < LANES
    index = jnp.bitwise_and(source, LANES - 1)
    turned = [
        jnp.take_along_axis(tile, index, axis=1, mode="promise_in_bounds")
        for tile in tiles[: count + 1]
    ]
    out = []
    for j in range(count):
        if j + 1 < len(turned):
            out.append(jnp.where(inside, turned[j], turned[j + 1]))
        else:
            out.append(turned[j])
    return out


def add_tiles(low, high):
    return [a + b for a, b in zip(low, high)]


def load_tiles(ref, rows, count):
    return [ref[rows, j * LANES : (j + 1) * LANES] for j in range(count)]


def load_strided(ref, rows, count):
    return [ref[j, rows, :] for j in range(count)]


def store_tiles(ref, row, tiles):
    for j, tile in enumerate(tiles):
        ref[row : row + GROUP, j * LANES : (j + 1) * LANES] = tile


def tile_count(length):
    return -(-length // LANES)


def window_kernel(n_z, block, x_ref, rim_ref, *rest):
    outs, joined = rest[:n_z], rest[n_z]
    samples = x_ref.shape[1]
    z = lax.axis_index("freq") // 2
    width = outs[0].shape[1]
    joined[:, :samples] = x_ref[...]
    joined[:, samples:] = rim_ref[...]
    for i in range(n_z):
        start = pl.multiple_of(jnp.bitwise_xor(z, i) * block, LANES)
        outs[i][...] = joined[:, pl.ds(start, width)]


def table_group(tab_ref, group):
    return tab_ref[group * GROUP : (group + 1) * GROUP, :]


def low_tree_kernel(n_z, counts, tab_ref, *rest):
    parts, out_ref, rows = rest[:n_z], rest[n_z], rest[n_z + 1]
    z = lax.axis_index("freq") // 2
    for i in range(n_z):
        where_z = jnp.bitwise_xor(z, i)
        value = parts[i][...]
        for q in range(2):
            start = pl.multiple_of((q * n_z + where_z) * GROUP, GROUP)
            for j in range(counts[0]):
                rows[j, pl.ds(start, GROUP), :] = value[:, j * LANES : (j + 1) * LANES]
    raw = [load_strided(rows, pl.ds(c, GROUP, stride=GROUP), counts[0]) for c in range(GROUP)]
    first = []
    for b in range(4):
        low = lane_shift(raw[2 * b], table_group(tab_ref, 2 * b), counts[1])
        for top in range(2):
            amount = table_group(tab_ref, 2 * b + 1) + table_group(tab_ref, 8 + 2 * b + top)
            first.append(add_tiles(low, lane_shift(raw[2 * b + 1], amount, counts[1])))
    second = []
    for b in range(2):
        for r in range(4):
            low, high = first[4 * b + r % 2], first[4 * b + 2 + r % 2]
            amount = table_group(tab_ref, 16 + 4 * b + r)
            second.append(add_tiles(low, lane_shift(high, amount, counts[2])))
    for r in range(8):
        low, high = second[r % 4], second[4 + r % 4]
        amount = table_group(tab_ref, 24 + r)
        store_tiles(out_ref, r * GROUP, add_tiles(low, lane_shift(high, amount, counts[3])))


def power_kernel(n_z, counts, taps, blocks, scale, tab_ref, mine_ref, theirs_ref, hi_ref, lo_ref, *rest):
    outs, rows, power = rest[:n_z], rest[n_z], rest[n_z + 1]
    z = lax.axis_index("freq") // 2
    lower_side = lax.axis_index("tm") == 0
    for r in range(8):
        mine = load_tiles(mine_ref, slice(r * GROUP, (r + 1) * GROUP), counts[0])
        theirs = load_tiles(theirs_ref, slice(r * GROUP, (r + 1) * GROUP), counts[0])
        low = [jnp.where(lower_side, a, b) for a, b in zip(mine, theirs)]
        high = [jnp.where(lower_side, b, a) for a, b in zip(mine, theirs)]
        amount = table_group(tab_ref, 32 + r)
        for j, tile in enumerate(add_tiles(low, lane_shift(high, amount, counts[1]))):
            rows[j, r * GROUP : (r + 1) * GROUP, :] = tile
    dedispersed = [None] * 8
    for half in range(2):
        band = [
            load_strided(rows, pl.ds(half * 4 * GROUP + s, GROUP, stride=4), counts[1])
            for s in range(4)
        ]
        fifth = []
        for b in range(2):
            for top in range(2):
                amount = table_group(tab_ref, 40 + 2 * (2 * b + top) + half)
                shifted = lane_shift(band[2 * b + 1], amount, counts[2])
                fifth.append(add_tiles(band[2 * b], shifted))
        for r in range(4):
            amount = table_group(tab_ref, 48 + 2 * r + half)
            shifted = lane_shift(fifth[2 + r % 2], amount, counts[3])
            dedispersed[2 * r + half] = add_tiles(fifth[r % 2], shifted)
    columns = [
        jnp.concatenate([dedispersed[g][j] for g in range(8)], axis=0) for j in range(counts[3])
    ]
    high_part = [c.astype(jnp.bfloat16) for c in columns]
    low_part = [
        (c - h.astype(jnp.float32)).astype(jnp.bfloat16) for c, h in zip(columns, high_part)
    ]

    def windows(part):
        return jnp.concatenate(
            [jnp.concatenate(part[m : m + 2], axis=1) for m in range(blocks)], axis=0
        )

    left_high, left_low = windows(high_part), windows(low_part)
    left = jnp.concatenate([left_high, left_low, left_high], axis=1)
    row_count = columns[0].shape[0]
    filters = hi_ref.shape[1] // LANES
    lane = lax.broadcasted_iota(jnp.int32, (row_count, LANES), 1)
    total = jnp.zeros((row_count, LANES), jnp.float32)
    for pair in range(filters // 2):
        cols = slice(pair * 2 * LANES, (pair + 1) * 2 * LANES)
        right = jnp.concatenate([hi_ref[:, cols], hi_ref[:, cols], lo_ref[:, cols]], axis=0)
        series = jnp.dot(left, right, preferred_element_type=jnp.float32)
        squares = series[:row_count] * series[:row_count]
        for m in range(1, blocks):
            piece = series[m * row_count : (m + 1) * row_count]
            squares = squares + piece * piece
        for f in range(2):
            energy = jnp.sum(squares[:, f * LANES : (f + 1) * LANES], axis=1, keepdims=True)
            total = jnp.where(lane == 2 * pair + f, energy * scale, total)
    power[...] = total
    for i in range(n_z):
        start = pl.multiple_of(jnp.bitwise_xor(z, i) * 2 * GROUP, 2 * GROUP)
        outs[i][...] = power[pl.ds(start, 2 * GROUP), :]


def toeplitz_kernel(bank_ref, hi_ref, lo_ref):
    filters, width = bank_ref.shape
    for f in range(filters):
        row = jnp.broadcast_to(bank_ref[f : f + 1, :], (width, width))
        turned = pltpu.roll(row, 0, 1, stride=1, stride_axis=0)[:, :LANES]
        high = turned.astype(jnp.bfloat16)
        hi_ref[:, f * LANES : (f + 1) * LANES] = high
        lo_ref[:, f * LANES : (f + 1) * LANES] = (turned - high.astype(jnp.float32)).astype(jnp.bfloat16)


def shift_tables(channel_shift, section_shift, core):
    by_channel = channel_shift.reshape(4, 2, 8, 2)
    by_section = section_shift[:4].reshape(4, 4, 2, 8, 2)
    low = jnp.concatenate([by_channel[None], by_section], axis=0)
    low = lax.dynamic_index_in_dim(low, core, 2, keepdims=False)
    low = jnp.transpose(low, (0, 2, 3, 1)).reshape(-1)
    high = section_shift[4:].reshape(2, 4, 2, 16)
    high = lax.dynamic_index_in_dim(high, core, 2, keepdims=False).reshape(-1)
    table = jnp.concatenate([low, high])
    return jnp.broadcast_to(table[:, None], (table.shape[0], LANES))


def swap_route(n_z, step):
    route = []
    for z in range(n_z):
        for x in range(2):
            for t in range(2):
                route.append((4 * z + 2 * x + t, 4 * (z ^ step) + 2 * t + x))
    return route


def swap_parts(parts):
    n_z = len(parts)
    return [lax.ppermute(parts[i], ("freq", "tm"), swap_route(n_z, i)) for i in range(n_z)]


def vmem(n):
    return [pl.BlockSpec(memory_space=pltpu.VMEM)] * n


def time_split_body(intensity, channel_shift, section_shift, filter_bank):
    chan_dev, samples = intensity.shape
    n_z = lax.axis_size("freq") // 2
    taps = filter_bank.shape[1]
    filters = filter_bank.shape[0]
    sections = section_shift.shape[0]
    span = samples // n_z
    halo = CHAN_MAX + SHIFT_UNIT * (2**sections - 1) + taps - 1
    rim = tile_count(halo) * LANES
    width = span + rim
    lengths = [span + halo]
    for section in range(sections):
        lengths.append(lengths[-1] - SHIFT_UNIT * 2**section - (CHAN_MAX if section == 0 else 0))
    counts = [tile_count(n) for n in lengths]
    core = lax.axis_index("tm")
    table = shift_tables(channel_shift, section_shift, core)
    f32, bf16 = jnp.float32, jnp.bfloat16
    bank = jnp.concatenate([filter_bank, jnp.zeros((filters, 2 * LANES - taps), f32)], axis=1)
    bank = jnp.roll(jnp.flip(bank, axis=1), 1, axis=1)
    high, low = pl.pallas_call(
        toeplitz_kernel,
        out_shape=[jax.ShapeDtypeStruct((2 * LANES, filters * LANES), bf16)] * 2,
        in_specs=vmem(1),
        out_specs=vmem(2),
    )(bank)
    rim_cols = from_behind(intensity[:, :rim], "tm", -1)
    parts = pl.pallas_call(
        partial(window_kernel, n_z, span),
        out_shape=[jax.ShapeDtypeStruct((chan_dev, width), f32)] * n_z,
        in_specs=vmem(2),
        out_specs=vmem(n_z),
        scratch_shapes=[pltpu.VMEM((chan_dev, samples + rim), f32)],
    )(intensity, rim_cols)
    parts = swap_parts(parts)
    mine = pl.pallas_call(
        partial(low_tree_kernel, n_z, counts[:4]),
        out_shape=jax.ShapeDtypeStruct((8 * GROUP, counts[3] * LANES), f32),
        in_specs=vmem(1 + n_z),
        out_specs=pl.BlockSpec(memory_space=pltpu.VMEM),
        scratch_shapes=[pltpu.VMEM((counts[0], 8 * GROUP, LANES), f32)],
    )(table, *parts)
    theirs = lax.ppermute(mine, "tm", [(0, 1), (1, 0)])
    scale = 1.0 / (BLOCK * chan_dev * 2 * n_z)
    pieces = pl.pallas_call(
        partial(power_kernel, n_z, counts[3:], taps, span // LANES, scale),
        out_shape=[jax.ShapeDtypeStruct((2 * GROUP, LANES), f32)] * n_z,
        in_specs=vmem(5),
        out_specs=vmem(n_z),
        scratch_shapes=[
            pltpu.VMEM((counts[4], 8 * GROUP, LANES), f32),
            pltpu.VMEM((8 * GROUP, LANES), f32),
        ],
    )(table, mine, theirs, high, low)
    pieces = swap_parts(pieces)
    z = lax.axis_index("freq") // 2
    ordered = []
    for block in range(n_z):
        step = jnp.bitwise_xor(z, block)
        value = pieces[0]
        for i in range(1, n_z):
            value = jnp.where(step == i, pieces[i], value)
        ordered.append(value[:, :filters])
    return jnp.stack(ordered, axis=2)


def fits_time_split(mesh, args):
    intensity, channel_shift, section_shift, filter_bank = args
    sizes = dict(mesh.shape)
    rows_dev = intensity.shape[0] // (sizes["beam"] * sizes["freq"])
    span = intensity.shape[1] // sizes["freq"]
    return (
        sizes["freq"] == 8
        and sizes["tm"] == 2
        and rows_dev == GROUP
        and channel_shift.shape[1] == 2
        and section_shift.shape[0] == 6
        and span == BLOCK
        and filter_bank.shape[1] <= LANES
        and filter_bank.shape[0] % 2 == 0
        and filter_bank.shape[0] <= GROUP
    )


def solution(mesh):
    in_specs = (P(("beam", "freq"), "tm"), P(), P(), P())
    out_specs = P(("beam", "freq"), None, "tm")

    def run(*args):
        chosen = time_split_body if fits_time_split(mesh, args) else body
        mapped = jax.shard_map(
            chosen, mesh=mesh, in_specs=in_specs, out_specs=out_specs, check_vma=False
        )
        return mapped(*args)

    return run
```
